1024 devices in a mesh: row: 32 (over z), col: 32 (over y, x, core).
Axes of the slice: x: 4, y: 4, z: 32, core: 2. Of those that a mesh axis runs over, the one named last changes fastest.
Arguments:
- volume: float32 [32, 32, 8, 24, 256], P('row', 'col'), may hold values from 0 to 2
- blocks_across: bfloat16 [32, 256, 256], replicated, may hold values from -0.375 to 0.375
- downward_ray_blocks: bfloat16 [32, 256, 256], replicated, may hold values from -0.375 to 0.375
- tiles_across: int32 [32, 32, 32], P('row', 'col'), may hold values from 0 to 7
- tiles_down: int32 [32, 32, 32], P('row', 'col'), may hold values from 0 to 7
- footprint_across: int32 [32, 32, 32], P('row', 'col'), may hold values from 64 to 256
- footprint_down: int32 [32, 32, 32], P('row', 'col'), may hold values from 64 to 256
- rays_across: int32 [32, 32, 32], P('row', 'col'), may hold values from 0 to 63, as said below
- rays_down: int32 [32, 32, 32], P('row', 'col'), may hold values from 0 to 63, as said below
- owners_across: int32 [32, 64], P('row'), may hold values from 0 to 63, as said below
- owners_down: int32 [32, 64], P('col'), may hold values from 0 to 63, as said below
- observed_sinogram_across: float32 [32, 32, 2, 24, 256], P('row', 'col'), may hold values from -24 to 24
- observed_sinogram_down: float32 [32, 32, 2, 24, 256], P('row', 'col'), may hold values from -24 to 24
- weights_across: float32 [32, 32, 2, 24, 256], P('row', 'col'), may hold values from 0.25 to 1
- weights_down: float32 [32, 32, 2, 24, 256], P('row', 'col'), may hold values from 0.25 to 1
Outputs:
- volume_out: float32 [32, 32, 8, 24, 256], P('row', 'col')
- residual_across: float32 [32, 32, 2, 24, 256], P('row', 'col')
- residual_down: float32 [32, 32, 2, 24, 256], P('row', 'col')
The draws below stay inside these ranges and needn't reach their ends.
Inputs may be any that keep to these rules, and one draw needn't show every extreme that they name: `rays_across`: ray ids are numbered within the device's row group. On one device no ray id appears twice, no owner column (owners_across[i, ray] // 2) is named by more than 2 slots, and on every device some owner column is named by exactly 2. `rays_down`: ray ids are numbered within the device's column group. On one device no ray id appears twice, no owner row (owners_down[j, ray] // 2) is named by more than 2 slots, and on every device some owner row is named by exactly 2. `owners_across`: each row is a permutation of 0 to 63. `owners_down`: each row is a permutation of 0 to 63.
All inputs are finite; a program needn't handle non-finite values.
Results may differ from the reference program's by a relative error of at most 0.028.
Values may be sent and summed in bfloat16 or wider, within the bound.
A program may use at most 32 MiB of HBM per device.

```python
import math
import jax
import jax.numpy as jnp
from jax import lax

TILE = 256
RAYS = 256
SLICES = 24
TILES_DEV = 8
OWNED = 2
ITERS = 2
SLOTS_ACROSS = 32
SLOTS_DOWN = 32
N_ROW = 32
N_COL = 32


def sender_slots(sender_key, peers):
    keys = jax.random.split(sender_key, 5)
    order = jax.random.permutation(keys[0], peers)
    pairs = jax.random.randint(keys[1], (), 1, peers // 2 + 1)
    places = jnp.arange(peers, dtype=jnp.int32)
    paired = places < 2 * pairs
    chosen = jnp.where(paired, places // 2, places - pairs)
    target = order[chosen]
    first_local = jax.random.randint(keys[2], (peers,), 0, OWNED)
    offsets = jax.random.randint(keys[3], (peers,), 1, OWNED)
    previous = jnp.roll(first_local, 1)
    second = paired & (places % 2 == 1)
    local_index = jnp.where(second, (previous + offsets) % OWNED, first_local)
    position = target * OWNED + local_index
    shuffle = jax.random.permutation(keys[4], peers)
    return position[shuffle]


def group_routes(group_key, peers):
    owner_key, slot_key = jax.random.split(group_key)
    owners = jax.random.permutation(owner_key, peers * OWNED).astype(jnp.int32)
    inverse = jnp.argsort(owners).astype(jnp.int32)
    sender_keys = jax.random.split(slot_key, peers)
    positions = jax.vmap(sender_slots, in_axes=(0, None))(sender_keys, peers)
    return (inverse[positions], owners)


def routing(key, groups, peers):
    group_keys = jax.random.split(key, groups)
    return jax.vmap(group_routes, in_axes=(0, None))(group_keys, peers)


def draw_rays_across(key, part):
    ray_ids, owners = routing(jax.random.fold_in(key, 11), N_ROW, N_COL)
    return ray_ids.astype(jnp.int32)


def draw_owners_across(key, part):
    ray_ids, owners = routing(jax.random.fold_in(key, 11), N_ROW, N_COL)
    return owners.astype(jnp.int32)


def draw_rays_down(key, part):
    ray_ids, owners = routing(jax.random.fold_in(key, 12), N_COL, N_ROW)
    return jnp.transpose(ray_ids, (1, 0, 2)).astype(jnp.int32)


def draw_owners_down(key, part):
    ray_ids, owners = routing(jax.random.fold_in(key, 12), N_COL, N_ROW)
    return owners.astype(jnp.int32)


def set_ends(array, own_key, smallest, top_value):
    longest = array.shape.index(max(array.shape))
    spots = []
    for shift in (0, 1):
        where = [jax.random.randint(jax.random.fold_in(own_key, axis), (), 0, length) for axis, length in enumerate(array.shape)]
        where[longest] = (where[longest] + shift) % array.shape[longest]
        spots.append(tuple(where))
    return array.at[spots[0]].set(smallest).at[spots[1]].set(top_value)


def shard_levels(key, shape, shards, least, largest):
    loudness = 1.0
    for dim, shards_of in shards:
        steps = jax.random.uniform(jax.random.fold_in(jax.random.fold_in(key, 6), dim), (shards_of,), jnp.float32, least / len(shards), largest / len(shards))
        loudness = loudness * jnp.repeat(jnp.exp(steps), shape[dim] // shards_of).reshape((-1,) + (1,) * (len(shape) - 1 - dim))
    return loudness


def normal_values(own_key, shape, deviation, bound, cuts=(), kind=jnp.bfloat16):
    entries = deviation * jax.random.normal(own_key, shape, jnp.float32)
    if cuts:
        entries = entries * shard_levels(own_key, shape, cuts, -0.22, 0.18)
    return jnp.clip(entries, -bound, bound).astype(kind)


def setup_inputs(seed: int = 0) -> dict:
    streams_of = jax.random.split(jax.random.key(seed), 16)
    return {
        "volume": jnp.clip(2.0 * jax.random.uniform(streams_of[0], (N_ROW, N_COL, TILES_DEV, SLICES, TILE), jnp.float32) ** shard_levels(streams_of[0], (N_ROW, N_COL, TILES_DEV, SLICES, TILE), ((0, 32), (1, 32)), -0.2, 0.2), 0.0, 2.0),
        "blocks_across": normal_values(streams_of[1], (SLOTS_ACROSS, TILE, RAYS), TILE ** -0.5, 0.375),
        "downward_ray_blocks": normal_values(streams_of[2], (SLOTS_DOWN, TILE, RAYS), TILE ** -0.5, 0.375),
        "tiles_across": set_ends(jax.random.randint(streams_of[3], (N_ROW, N_COL, SLOTS_ACROSS), 0, TILES_DEV), jax.random.fold_in(streams_of[3], 1), 0, TILES_DEV - 1).astype(jnp.int32),
        "tiles_down": set_ends(jax.random.randint(streams_of[4], (N_ROW, N_COL, SLOTS_DOWN), 0, TILES_DEV), jax.random.fold_in(streams_of[4], 1), 0, TILES_DEV - 1).astype(jnp.int32),
        "footprint_across": set_ends(jax.random.randint(streams_of[5], (N_ROW, N_COL, SLOTS_ACROSS), RAYS // 4, RAYS + 1), jax.random.fold_in(streams_of[5], 1), RAYS // 4, RAYS).astype(jnp.int32),
        "footprint_down": set_ends(jax.random.randint(streams_of[6], (N_ROW, N_COL, SLOTS_DOWN), RAYS // 4, RAYS + 1), jax.random.fold_in(streams_of[6], 1), RAYS // 4, RAYS).astype(jnp.int32),
        "rays_across": draw_rays_across(jax.random.fold_in(streams_of[15], 71), 0),
        "rays_down": draw_rays_down(jax.random.fold_in(streams_of[15], 71), 0),
        "owners_across": draw_owners_across(jax.random.fold_in(streams_of[15], 71), 0),
        "owners_down": draw_owners_down(jax.random.fold_in(streams_of[15], 71), 0),
        "observed_sinogram_across": normal_values(streams_of[11], (N_ROW, N_COL, OWNED, SLICES, RAYS), 4.0, 24.0, ((0, 32), (1, 32)), jnp.float32),
        "observed_sinogram_down": normal_values(streams_of[12], (N_ROW, N_COL, OWNED, SLICES, RAYS), 4.0, 24.0, ((0, 32), (1, 32)), jnp.float32),
        "weights_across": jnp.clip(jnp.exp(math.log(1.0) - 1.3862944 * jax.random.uniform(streams_of[13], (N_ROW, N_COL, OWNED, SLICES, RAYS), jnp.float32) ** shard_levels(streams_of[13], (N_ROW, N_COL, OWNED, SLICES, RAYS), ((0, 32), (1, 32)), -0.2, 0.2)), 0.25, 1.0),
        "weights_down": jnp.clip(jnp.exp(math.log(1.0) - 1.3862944 * jax.random.uniform(streams_of[14], (N_ROW, N_COL, OWNED, SLICES, RAYS), jnp.float32) ** shard_levels(streams_of[14], (N_ROW, N_COL, OWNED, SLICES, RAYS), ((0, 32), (1, 32)), -0.2, 0.2)), 0.25, 1.0),
    }


HUBER_DELTA = 0.5
STEP_SIZE = 0.05
SMOOTH_WEIGHT = 1.0


def take_tiles(tile_stack, tile_list):
    return jnp.take(tile_stack, tile_list, axis=0)


def take_entries(table, index_list):
    return jnp.take(table, index_list, axis=0)


def forward_family(volume_bf, blocks, tiles, footprint):
    blocks_f = blocks.astype(jnp.float32)
    ray_index = jnp.arange(blocks.shape[2], dtype=jnp.int32)

    def per_row(row_args):
        volume_row, tile_row, foot_row = row_args
        chosen = jax.vmap(take_tiles)(volume_row, tile_row).astype(jnp.float32)
        partial_value = jnp.einsum("csvt,str->csvr", chosen, blocks_f)
        keep = ray_index[None, None, :] < foot_row[:, :, None]
        return jnp.where(keep[:, :, None, :], partial_value, 0.0).astype(jnp.bfloat16)

    return lax.map(per_row, (volume_bf, tiles, footprint))


def backward_family(items, blocks, tiles, footprint, num_tiles):
    blocks_f = blocks.astype(jnp.float32)
    ray_index = jnp.arange(blocks.shape[2], dtype=jnp.int32)
    tile_index = jnp.arange(num_tiles, dtype=jnp.int32)

    def per_row(row_args):
        item_row, tile_row, foot_row = row_args
        keep = ray_index[None, None, :] < foot_row[:, :, None]
        masked = jnp.where(keep[:, :, None, :], item_row.astype(jnp.float32), 0.0)
        contrib = jnp.einsum("csvr,str->csvt", masked, blocks_f)
        tile_pick = (tile_row[:, :, None] == tile_index[None, None, :]).astype(jnp.float32)
        return jnp.einsum("csk,csvt->ckvt", tile_pick, contrib, precision=lax.Precision.HIGHEST)

    return lax.map(per_row, (items, tiles, footprint))


def ray_totals(partials, segment):
    flat = partials.reshape(-1, SLICES * RAYS).astype(jnp.float32)
    total = jax.ops.segment_sum(flat, segment.reshape(-1), num_segments=N_ROW * N_COL * OWNED)
    return total.reshape(N_ROW, N_COL, OWNED, SLICES, RAYS)


def spread_back(residual_bf, segment, shape):
    flat = residual_bf.reshape(-1, SLICES, RAYS)
    return jnp.take(flat, segment.reshape(-1), axis=0).reshape(shape)


def smooth_gradient(voxels):
    diff = voxels[..., 1:, :] - voxels[..., :-1, :]
    slope = jnp.clip(diff, -HUBER_DELTA, HUBER_DELTA)
    zero_row = jnp.zeros_like(slope[..., :1, :])
    return jnp.concatenate([zero_row, slope], axis=-2) - jnp.concatenate([slope, zero_row], axis=-2)


def reference(volume, blocks_across, downward_ray_blocks, tiles_across, tiles_down, footprint_across, footprint_down, rays_across, rays_down, owners_across, owners_down, observed_sinogram_across, observed_sinogram_down, weights_across, weights_down):
    num_tiles = volume.shape[2]
    slots_a = rays_across.shape[2]
    slots_d = rays_down.shape[2]
    row_index = jnp.arange(N_ROW, dtype=jnp.int32)
    col_index = jnp.arange(N_COL, dtype=jnp.int32)
    pos_across = jax.vmap(take_entries)(owners_across, rays_across.reshape(N_ROW, N_COL * slots_a)).reshape(N_ROW, N_COL, slots_a)
    seg_across = row_index[:, None, None] * (N_COL * OWNED) + pos_across
    down_t = jnp.transpose(rays_down, (1, 0, 2)).reshape(N_COL, N_ROW * slots_d)
    pos_down = jnp.transpose(jax.vmap(take_entries)(owners_down, down_t).reshape(N_COL, N_ROW, slots_d), (1, 0, 2))
    seg_down = (pos_down // OWNED) * (N_COL * OWNED) + col_index[None, :, None] * OWNED + pos_down % OWNED
    voxels = volume
    misfit_across_rays = observed_sinogram_across
    misfit_down_rays = observed_sinogram_down
    for iteration in range(ITERS):
        volume_bf = voxels.astype(jnp.bfloat16)
        part_across = forward_family(volume_bf, blocks_across, tiles_across, footprint_across)
        part_down = forward_family(volume_bf, downward_ray_blocks, tiles_down, footprint_down)
        misfit_across_rays = weights_across * (observed_sinogram_across - ray_totals(part_across, seg_across))
        misfit_down_rays = weights_down * (observed_sinogram_down - ray_totals(part_down, seg_down))
        items_across = spread_back(misfit_across_rays.astype(jnp.bfloat16), seg_across, part_across.shape)
        items_down = spread_back(misfit_down_rays.astype(jnp.bfloat16), seg_down, part_down.shape)
        gradient = backward_family(items_across, blocks_across, tiles_across, footprint_across, num_tiles)
        gradient = gradient + backward_family(items_down, downward_ray_blocks, tiles_down, footprint_down, num_tiles)
        voxels = jnp.maximum(voxels + STEP_SIZE * (gradient - SMOOTH_WEIGHT * smooth_gradient(voxels)), 0.0)
    return voxels, misfit_across_rays, misfit_down_rays
```

```python
import functools

import jax
import jax.numpy as jnp
from jax import lax
from jax.experimental import pallas as pl
from jax.experimental.pallas import tpu as pltpu
from jax.sharding import PartitionSpec as P

OWNED = 2
ITERS = 2
RING = 4

HUBER_DELTA = 0.5
STEP_SIZE = 0.05
SMOOTH_WEIGHT = 1.0

F32 = jnp.float32
BF16 = jnp.bfloat16

SLOT, TILE_OF, FOOT, OWNER, ODD, SAME, INVERSE, LAST = range(8)


def slot_tables(ray_list, owner_row, tiles, footprint, num_tiles):
    positions = owner_row.shape[0]
    slots = ray_list.shape[0]
    ids = jnp.arange(slots, dtype=jnp.int32)
    earlier = ids[None, :] < ids[:, None]
    before = (tiles[None, :] < tiles[:, None]) | ((tiles[None, :] == tiles[:, None]) & earlier)
    rank = jnp.sum(before.astype(jnp.int32), axis=1)
    named = ray_list[:, None] == jnp.arange(positions, dtype=jnp.int32)[None, :]
    position = jnp.sum(jnp.where(named, owner_row[None, :], 0), axis=1)
    here = rank[None, :] == ids[:, None]

    def sort(values):
        return jnp.sum(jnp.where(here, values[None, :], 0), axis=1)

    slot = sort(ids)
    tile = sort(tiles)
    foot = sort(footprint)
    pos = sort(position)
    same = jnp.concatenate([jnp.zeros((1,), jnp.int32), (tile[1:] == tile[:-1]).astype(jnp.int32)])
    holds = pos[None, :] == jnp.arange(positions, dtype=jnp.int32)[:, None]
    inverse = slots - jnp.sum(jnp.where(holds, slots - ids[None, :], 0), axis=1)
    tile_ids = jnp.arange(num_tiles, dtype=jnp.int32)
    upto = jnp.sum((tiles[None, :] <= tile_ids[:, None]).astype(jnp.int32), axis=1)
    present = jnp.any(tiles[None, :] == tile_ids[:, None], axis=1)
    last = jnp.where(present, upto - 1, slots)
    width = max(positions, slots, num_tiles)

    def row(values):
        return jnp.pad(values.astype(jnp.int32), (0, width - values.shape[0]))

    return jnp.stack(
        [row(v) for v in (slot, tile, foot, pos // OWNED, pos % OWNED, same, inverse, last)]
    )


def body(
    n_row,
    n_col,
    tab_a,
    tab_d,
    vol,
    blk_a_hbm,
    blk_d_hbm,
    meas_a,
    meas_d,
    wt_a,
    wt_d,
    vol_out,
    res_a,
    res_d,
    blk_a,
    blk_d,
    part_a,
    part_d,
    cum_a,
    cum_d,
    smooth,
    gat_a,
    gat_d,
    send_a,
    recv_a,
    sp,
    rp,
    sm,
    rm,
    hub,
    half_s,
    half_r,
    full_s,
    full_r,
    blk_sem,
    ca_s,
    ca_r,
    cg_s,
    cg_r,
    sp_s,
    sp_r,
    sm_s,
    sm_r,
    h_s,
    h_r,
    f_s,
    f_r,
    gf_s,
    gf_r,
    gh_s,
    gh_r,
    gp_s,
    gp_r,
    gm_s,
    gm_r,
):
    z = lax.axis_index("row")
    c = lax.axis_index("col")
    num_tiles, slices, _ = vol.shape
    slots_a = blk_a.shape[0]
    slots_d = blk_d.shape[0]
    rays = blk_a.shape[2]
    lanes = rays // 2
    gap = n_row // RING
    up_steps = gap // 2
    down_steps = gap // 2 - 1

    def zrow(offset):
        return lax.rem(z + (offset % n_row), n_row)

    def zdev(offset):
        return (zrow(offset), c)

    def ccol(k):
        return lax.rem(c + k, n_col)

    def remote(src, dst, s_sem, r_sem, dev):
        return pltpu.make_async_remote_copy(
            src_ref=src,
            dst_ref=dst,
            send_sem=s_sem,
            recv_sem=r_sem,
            device_id=dev,
            device_id_type=pl.DeviceIdType.MESH,
        )

    loads = (
        pltpu.make_async_copy(blk_d_hbm, blk_d, blk_sem.at[0]),
        pltpu.make_async_copy(blk_a_hbm, blk_a, blk_sem.at[1]),
    )
    for load in loads:
        load.start()

    barrier = pltpu.get_barrier_semaphore()

    def greet(k, carry):
        pl.semaphore_signal(
            barrier, inc=1, device_id=(z, ccol(k)), device_id_type=pl.DeviceIdType.MESH
        )
        return carry

    for offset in (gap, -gap, 1, -1):
        pl.semaphore_signal(
            barrier, inc=1, device_id=zdev(offset), device_id_type=pl.DeviceIdType.MESH
        )
    lax.fori_loop(1, n_col, greet, 0)

    zero = jnp.zeros((slices, rays), F32)
    part_a[slots_a] = zero
    part_d[slots_d] = zero
    cum_a[slots_a] = zero
    cum_d[slots_d] = zero
    for k in range(num_tiles):
        vol_out[k] = vol[k]

    ray_index = lax.broadcasted_iota(jnp.int32, (slices, rays), 1)
    slice_index = lax.broadcasted_iota(jnp.int32, (slices, rays), 0)

    def forward(tab, blk, part, first, count):
        def one(j, carry):
            tile = vol_out[tab[TILE_OF, j]].astype(BF16)
            value = jnp.dot(tile, blk[tab[SLOT, j]], preferred_element_type=F32)
            part[j] = jnp.where(ray_index < tab[FOOT, j], value, 0.0)
            return carry

        lax.fori_loop(first, first + count, one, 0, unroll=min(4, count))

    def backward(tab, blk, gat, cum, first, count):
        def one(j, total):
            both = gat[tab[OWNER, j]].astype(F32)
            items = jnp.where(tab[ODD, j] == 1, both[slices:], both[:slices])
            items = jnp.where(ray_index < tab[FOOT, j], items, 0.0).astype(BF16)
            value = lax.dot_general(
                items, blk[tab[SLOT, j]], (((1,), (1,)), ((), ())), preferred_element_type=F32
            )
            total = jnp.where(tab[SAME, j] == 1, total, 0.0) + value
            cum[j] = total
            return total

        start = cum[first - 1] if first else zero
        lax.fori_loop(first, first + count, one, start, unroll=min(4, count))

    def own(tab, part, owner):
        return jnp.concatenate(
            [part[tab[INVERSE, 2 * owner]], part[tab[INVERSE, 2 * owner + 1]]], axis=0
        )

    def own_d(owner):
        return own(tab_d, part_d, owner)

    def own_a(owner):
        return own(tab_a, part_a, owner)

    def smoothing():
        for k in range(num_tiles):
            x = vol_out[k]
            step = pltpu.roll(x, slices - 1, 0) - x
            slope = jnp.clip(step, -HUBER_DELTA, HUBER_DELTA)
            slope = jnp.where(slice_index < slices - 1, slope, 0.0)
            smooth[k] = pltpu.roll(slope, 1, 0) - slope

    parts = 4
    per = slots_a // parts if slots_a % parts == 0 else slots_a

    def pieces(fn):
        return [functools.partial(fn, i * per, per) for i in range(slots_a // per)]

    def send_across():
        def one(k, carry):
            send_a[k] = own_a(ccol(k)).astype(BF16)
            remote(send_a.at[k], recv_a.at[k], ca_s.at[k], ca_r.at[k], (z, ccol(k))).start()
            return carry

        lax.fori_loop(1, n_col, one, 0)

    def finish_across():
        def one(k, total):
            remote(send_a.at[k], recv_a.at[k], ca_s.at[k], ca_r.at[k], (z, ccol(k))).wait_recv()
            return total + recv_a[k].astype(F32)

        projection = lax.fori_loop(1, n_col, one, own_a(c))
        residual = wt_a[...] * (meas_a[...] - projection)
        res_a[...] = residual
        gat_a[c] = residual.astype(BF16)

        def spread(k, carry):
            remote(gat_a.at[c], gat_a.at[c], cg_s.at[k], cg_r.at[k], (z, ccol(k))).start()
            return carry

        lax.fori_loop(1, n_col, spread, 0)

    def collect_across():
        def one(k, carry):
            remote(gat_a.at[c], gat_a.at[c], cg_s.at[k], cg_r.at[k], (z, ccol(k))).wait_recv()
            return carry

        lax.fori_loop(1, n_col, one, 0)

    def drain_across():
        def one(k, carry):
            remote(send_a.at[k], recv_a.at[k], ca_s.at[k], ca_r.at[k], (z, ccol(k))).wait_send()
            remote(gat_a.at[c], gat_a.at[c], cg_s.at[k], cg_r.at[k], (z, ccol(k))).wait_send()
            return carry

        lax.fori_loop(1, n_col, one, 0)

    def plus(t, k):
        return remote(sp.at[t, k], rp.at[t, k], sp_s.at[t, k], sp_r.at[t, k], zdev(1))

    def minus(t, k):
        return remote(sm.at[t, k], rm.at[t, k], sm_s.at[t, k], sm_r.at[t, k], zdev(-1))

    def half(i):
        return remote(half_s.at[i], half_r.at[i], h_s.at[i], h_r.at[i], zdev(gap if i == 0 else -gap))

    def full(i):
        return remote(full_s.at[i], full_r.at[i], f_s.at[i], f_r.at[i], zdev(gap if i == 0 else -gap))

    def chain_step(t, k):
        value = own_d(zrow(up_steps - t + gap * k))
        if t:
            plus(t - 1, k).wait_recv()
            value = value + rp[t - 1, k].astype(F32)
        sp[t, k] = value.astype(BF16)
        plus(t, k).start()
        if t < down_steps:
            value = own_d(zrow(t - down_steps + gap * k))
            if t:
                minus(t - 1, k).wait_recv()
                value = value + rm[t - 1, k].astype(F32)
            sm[t, k] = value.astype(BF16)
            minus(t, k).start()

    def hub_total(k):
        value = own_d(zrow(gap * k))
        if down_steps:
            minus(down_steps - 1, k).wait_recv()
            value = value + rm[down_steps - 1, k].astype(F32)
        plus(up_steps - 1, k).wait_recv()
        return value + rp[up_steps - 1, k].astype(F32)

    def reduce_down(fillers):
        fillers = list(fillers)
        for t in range(up_steps):
            for k in (2, 1, 3):
                chain_step(t, k)
            if fillers:
                fillers.pop(0)()
        value = hub_total(2)
        half_s[0] = value[:, :lanes].astype(BF16)
        half_s[1] = value[:, lanes:].astype(BF16)
        half(0).start()
        half(1).start()
        for filler in fillers:
            filler()
        send_across()
        hub[0] = hub_total(1)
        hub[1] = hub_total(3)
        for t in range(up_steps):
            chain_step(t, 0)
        smoothing()
        hub[2] = hub_total(0)
        half(0).wait_recv()
        value = hub[0]
        full_s[0, :, :lanes] = (value[:, :lanes] + half_r[0].astype(F32)).astype(BF16)
        full_s[0, :, lanes:] = value[:, lanes:].astype(BF16)
        full(0).start()
        half(1).wait_recv()
        value = hub[1]
        full_s[1, :, :lanes] = value[:, :lanes].astype(BF16)
        full_s[1, :, lanes:] = (value[:, lanes:] + half_r[1].astype(F32)).astype(BF16)
        full(1).start()
        finish_across()
        full(0).wait_recv()
        full(1).wait_recv()
        projection = hub[2] + full_r[0].astype(F32) + full_r[1].astype(F32)
        residual = wt_d[...] * (meas_d[...] - projection)
        res_d[...] = residual
        gat_d[z] = residual.astype(BF16)

    def out_full(i, offset):
        mine = gat_d.at[zrow(offset)]
        return remote(mine, mine, gf_s.at[i], gf_r.at[i], zdev(gap if i == 0 else -gap))

    def out_half(i):
        owner = zrow(-gap if i == 0 else gap)
        piece = gat_d.at[owner, :, pl.ds(i * lanes, lanes)]
        return remote(piece, piece, gh_s.at[i], gh_r.at[i], zdev(gap if i == 0 else -gap))

    def out_minus(t, k):
        shard = gat_d.at[zrow(t + gap * k)]
        return remote(shard, shard, gm_s.at[t, k], gm_r.at[t, k], zdev(-1))

    def out_plus(t, k):
        shard = gat_d.at[zrow(gap * k - t)]
        return remote(shard, shard, gp_s.at[t, k], gp_r.at[t, k], zdev(1))

    def out_step(t, k):
        if t:
            out_minus(t - 1, k).wait_recv()
        out_minus(t, k).start()
        if t < down_steps:
            if t:
                out_plus(t - 1, k).wait_recv()
            out_plus(t, k).start()

    def out_last(k):
        out_minus(up_steps - 1, k).wait_recv()
        if down_steps:
            out_plus(down_steps - 1, k).wait_recv()

    def spread_down(fillers):
        fillers = list(fillers)
        out_full(0, 0).start()
        out_full(1, 0).start()
        for t in range(up_steps):
            out_step(t, 0)
        out_full(0, 0).wait_recv()
        out_half(0).start()
        out_full(1, 0).wait_recv()
        out_half(1).start()
        for k in (1, 3):
            out_step(0, k)
        collect_across()
        for t in range(1, up_steps):
            if fillers:
                fillers.pop(0)()
            for k in (1, 3):
                out_step(t, k)
        for filler in fillers:
            filler()
        out_half(0).wait_recv()
        out_half(1).wait_recv()
        for t in range(up_steps):
            out_step(t, 2)
        for k in (0, 1, 3, 2):
            out_last(k)

    def drain_down():
        for k in range(RING):
            for t in range(up_steps):
                plus(t, k).wait_send()
                out_minus(t, k).wait_send()
            for t in range(down_steps):
                minus(t, k).wait_send()
                out_plus(t, k).wait_send()
        for i in range(2):
            half(i).wait_send()
            full(i).wait_send()
            out_full(i, 0).wait_send()
            out_half(i).wait_send()

    loads[0].wait()
    forward(tab_d, blk_d, part_d, 0, slots_d)
    loads[1].wait()
    pl.semaphore_wait(barrier, n_col - 1 + 4)

    def iteration(step, carry):
        reduce_down(pieces(functools.partial(forward, tab_a, blk_a, part_a)))
        spread_down(pieces(functools.partial(backward, tab_a, blk_a, gat_a, cum_a)))
        backward(tab_d, blk_d, gat_d, cum_d, 0, slots_d)
        for k in range(num_tiles):
            gradient = cum_a[tab_a[LAST, k]] + cum_d[tab_d[LAST, k]]
            x = vol_out[k]
            vol_out[k] = jnp.maximum(
                x + STEP_SIZE * (gradient - SMOOTH_WEIGHT * smooth[k]), 0.0
            )
        drain_across()
        drain_down()

        @pl.when(step < ITERS - 1)
        def _():
            forward(tab_d, blk_d, part_d, 0, slots_d)

        return carry

    lax.fori_loop(0, ITERS, iteration, 0)


def shards(
    n_row,
    n_col,
    volume,
    blocks_across,
    downward_ray_blocks,
    tiles_across,
    tiles_down,
    footprint_across,
    footprint_down,
    rays_across,
    rays_down,
    owners_across,
    owners_down,
    observed_sinogram_across,
    observed_sinogram_down,
    weights_across,
    weights_down,
):
    voxels = volume[0, 0]
    num_tiles, slices, tile = voxels.shape
    slots_a, _, rays = blocks_across.shape
    slots_d = downward_ray_blocks.shape[0]
    rows = OWNED * slices
    tab_a = slot_tables(
        rays_across[0, 0], owners_across[0], tiles_across[0, 0], footprint_across[0, 0], num_tiles
    )
    tab_d = slot_tables(
        rays_down[0, 0], owners_down[0], tiles_down[0, 0], footprint_down[0, 0], num_tiles
    )
    gap = n_row // RING
    up_steps = gap // 2
    down_steps = max(gap // 2 - 1, 1)
    dma = pltpu.SemaphoreType.DMA

    def shard(*lead):
        return pltpu.VMEM((*lead, rows, rays), BF16)

    vmem = pl.BlockSpec(memory_space=pltpu.VMEM)
    smem = pl.BlockSpec(memory_space=pltpu.SMEM)
    anywhere = pl.BlockSpec(memory_space=pl.ANY)
    own_shape = jax.ShapeDtypeStruct((rows, rays), F32)
    outs = pl.pallas_call(
        functools.partial(body, n_row, n_col),
        out_shape=(jax.ShapeDtypeStruct(voxels.shape, F32), own_shape, own_shape),
        in_specs=[smem, smem, vmem, anywhere, anywhere, vmem, vmem, vmem, vmem],
        out_specs=(vmem, vmem, vmem),
        scratch_shapes=[
            pltpu.VMEM(blocks_across.shape, BF16),
            pltpu.VMEM(downward_ray_blocks.shape, BF16),
            pltpu.VMEM((slots_a + 1, slices, rays), F32),
            pltpu.VMEM((slots_d + 1, slices, rays), F32),
            pltpu.VMEM((slots_a + 1, slices, tile), F32),
            pltpu.VMEM((slots_d + 1, slices, tile), F32),
            pltpu.VMEM(voxels.shape, F32),
            shard(n_col),
            shard(n_row),
            shard(n_col),
            shard(n_col),
            shard(up_steps, RING),
            shard(up_steps, RING),
            shard(down_steps, RING),
            shard(down_steps, RING),
            pltpu.VMEM((3, rows, rays), F32),
            pltpu.VMEM((2, rows, rays // 2), BF16),
            pltpu.VMEM((2, rows, rays // 2), BF16),
            shard(2),
            shard(2),
            dma((2,)),
            dma((n_col,)),
            dma((n_col,)),
            dma((n_col,)),
            dma((n_col,)),
            dma((up_steps, RING)),
            dma((up_steps, RING)),
            dma((down_steps, RING)),
            dma((down_steps, RING)),
            dma((2,)),
            dma((2,)),
            dma((2,)),
            dma((2,)),
            dma((2,)),
            dma((2,)),
            dma((2,)),
            dma((2,)),
            dma((down_steps, RING)),
            dma((down_steps, RING)),
            dma((up_steps, RING)),
            dma((up_steps, RING)),
        ],
        compiler_params=pltpu.CompilerParams(
            collective_id=0, has_side_effects=True, vmem_limit_bytes=48 << 20
        ),
        name="tomography",
    )(
        tab_a,
        tab_d,
        voxels,
        blocks_across,
        downward_ray_blocks,
        observed_sinogram_across.reshape(rows, rays),
        observed_sinogram_down.reshape(rows, rays),
        weights_across.reshape(rows, rays),
        weights_down.reshape(rows, rays),
    )
    shape = observed_sinogram_across.shape
    return (outs[0][None, None], outs[1].reshape(shape), outs[2].reshape(shape))


def solution(mesh):
    return jax.shard_map(
        functools.partial(shards, mesh.shape["row"], mesh.shape["col"]),
        mesh=mesh,
        in_specs=(
            P("row", "col", None, None, None),
            P(),
            P(),
            P("row", "col", None),
            P("row", "col", None),
            P("row", "col", None),
            P("row", "col", None),
            P("row", "col", None),
            P("row", "col", None),
            P("row", None),
            P("col", None),
            P("row", "col", None, None, None),
            P("row", "col", None, None, None),
            P("row", "col", None, None, None),
            P("row", "col", None, None, None),
        ),
        out_specs=(
            P("row", "col", None, None, None),
            P("row", "col", None, None, None),
            P("row", "col", None, None, None),
        ),
        check_vma=False,
    )
```

```python
import functools

import jax
import jax.numpy as jnp
from jax import lax
from jax.experimental import pallas as pl
from jax.experimental.pallas import tpu as pltpu
from jax.sharding import PartitionSpec as P

OWNED = 2
ITERS = 2
RING = 4

HUBER_DELTA = 0.5
STEP_SIZE = 0.05
SMOOTH_WEIGHT = 1.0

F32 = jnp.float32
BF16 = jnp.bfloat16

SLOT, TILE_OF, FOOT, OWNER, ODD, SAME, INVERSE, LAST = range(8)


def slot_tables(num_tiles, ray_list, owner_row, tiles, footprint):
    positions = owner_row.shape[0]
    slots = ray_list.shape[0]
    ids = jnp.arange(slots, dtype=jnp.int32)
    earlier = ids[None, :] < ids[:, None]
    before = (tiles[None, :] < tiles[:, None]) | ((tiles[None, :] == tiles[:, None]) & earlier)
    rank = jnp.sum(before.astype(jnp.int32), axis=1)
    named = ray_list[:, None] == jnp.arange(positions, dtype=jnp.int32)[None, :]
    position = jnp.sum(jnp.where(named, owner_row[None, :], 0), axis=1)
    here = rank[None, :] == ids[:, None]

    def sort(values):
        return jnp.sum(jnp.where(here, values[None, :], 0), axis=1)

    slot = sort(ids)
    tile = sort(tiles)
    foot = sort(footprint)
    pos = sort(position)
    same = jnp.concatenate([jnp.zeros((1,), jnp.int32), (tile[1:] == tile[:-1]).astype(jnp.int32)])
    holds = pos[None, :] == jnp.arange(positions, dtype=jnp.int32)[:, None]
    inverse = slots - jnp.sum(jnp.where(holds, slots - ids[None, :], 0), axis=1)
    tile_ids = jnp.arange(num_tiles, dtype=jnp.int32)
    upto = jnp.sum((tiles[None, :] <= tile_ids[:, None]).astype(jnp.int32), axis=1)
    present = jnp.any(tiles[None, :] == tile_ids[:, None], axis=1)
    last = jnp.where(present, upto - 1, slots)
    width = max(positions, slots, num_tiles)

    def row(values):
        return jnp.pad(values.astype(jnp.int32), (0, width - values.shape[0]))

    return jnp.stack(
        [row(v) for v in (slot, tile, foot, pos // OWNED, pos % OWNED, same, inverse, last)]
    )


def body(
    n_row,
    n_col,
    tab_a,
    tab_d,
    vol,
    blk_a_hbm,
    blk_d_hbm,
    meas_a_hbm,
    meas_d_hbm,
    wt_a_hbm,
    wt_d_hbm,
    vol_out,
    res_a,
    res_d,
    blk_a,
    blk_d,
    meas_a,
    meas_d,
    wt_a,
    wt_d,
    part_a,
    part_d,
    cum_a,
    cum_d,
    smooth,
    gat_a,
    gat_d,
    twin_s,
    twin_r,
    send_a,
    recv_a,
    sp,
    rp,
    sm,
    rm,
    hub,
    half_s,
    half_r,
    full_s,
    full_r,
    blk_sem,
    tw_s,
    tw_r,
    tg_s,
    tg_r,
    ca_s,
    ca_r,
    cg_s,
    cg_r,
    sp_s,
    sp_r,
    sm_s,
    sm_r,
    h_s,
    h_r,
    f_s,
    f_r,
    gf_s,
    gf_r,
    gh_s,
    gh_r,
    gp_s,
    gp_r,
    gm_s,
    gm_r,
):
    z = lax.axis_index("row")
    c = lax.axis_index("col")
    num_tiles, slices, _ = vol.shape
    slots_a = blk_a.shape[0]
    slots_d = blk_d.shape[0]
    rays = blk_a.shape[2]
    lanes = rays // 2
    gap = n_row // RING
    up_steps = gap // 2
    down_steps = gap // 2 - 1

    def zrow(offset):
        return lax.rem(z + (offset % n_row), n_row)

    def zdev(offset):
        return (zrow(offset), c)

    chips = n_col // 2
    core = lax.rem(c, 2)
    chip = (c - core) // 2
    twin = (z, c + 1 - 2 * core)

    def ccol(k, side):
        return 2 * lax.rem(chip + k, chips) + side

    def cdev(k):
        return (z, ccol(k, core))

    def remote(src, dst, s_sem, r_sem, dev):
        return pltpu.make_async_remote_copy(
            src_ref=src,
            dst_ref=dst,
            send_sem=s_sem,
            recv_sem=r_sem,
            device_id=dev,
            device_id_type=pl.DeviceIdType.MESH,
        )

    pairs = (
        (vol, vol_out),
        (blk_d_hbm, blk_d),
        (blk_a_hbm, blk_a),
        (meas_d_hbm, meas_d),
        (wt_d_hbm, wt_d),
        (meas_a_hbm, meas_a),
        (wt_a_hbm, wt_a),
    )
    loads = [pltpu.make_async_copy(src, dst, blk_sem.at[i]) for i, (src, dst) in enumerate(pairs)]
    for load in loads:
        load.start()

    barrier = pltpu.get_barrier_semaphore()

    def greet(k, carry):
        pl.semaphore_signal(
            barrier, inc=1, device_id=cdev(k), device_id_type=pl.DeviceIdType.MESH
        )
        return carry

    for offset in (gap, -gap, 1, -1):
        pl.semaphore_signal(
            barrier, inc=1, device_id=zdev(offset), device_id_type=pl.DeviceIdType.MESH
        )
    pl.semaphore_signal(barrier, inc=1, device_id=twin, device_id_type=pl.DeviceIdType.MESH)
    lax.fori_loop(1, chips, greet, 0)

    zero = jnp.zeros((slices, rays), F32)
    part_a[slots_a] = zero
    part_d[slots_d] = zero
    cum_a[slots_a] = zero
    cum_d[slots_d] = zero

    ray_index = lax.broadcasted_iota(jnp.int32, (slices, rays), 1)
    slice_index = lax.broadcasted_iota(jnp.int32, (slices, rays), 0)

    def forward(tab, blk, part, first, count):
        def one(j, carry):
            tile = vol_out[tab[TILE_OF, j]].astype(BF16)
            value = jnp.dot(tile, blk[tab[SLOT, j]], preferred_element_type=F32)
            part[j] = jnp.where(ray_index < tab[FOOT, j], value, 0.0)
            return carry

        lax.fori_loop(first, first + count, one, 0, unroll=min(4, count))

    def backward(tab, blk, gat, cum, first, count):
        def one(j, total):
            both = gat[tab[OWNER, j]].astype(F32)
            items = jnp.where(tab[ODD, j] == 1, both[slices:], both[:slices])
            items = jnp.where(ray_index < tab[FOOT, j], items, 0.0).astype(BF16)
            value = lax.dot_general(
                items, blk[tab[SLOT, j]], (((1,), (1,)), ((), ())), preferred_element_type=F32
            )
            total = jnp.where(tab[SAME, j] == 1, total, 0.0) + value
            cum[j] = total
            return total

        start = cum[first - 1] if first else zero
        lax.fori_loop(first, first + count, one, start, unroll=min(4, count))

    def own(tab, part, owner):
        return jnp.concatenate(
            [part[tab[INVERSE, 2 * owner]], part[tab[INVERSE, 2 * owner + 1]]], axis=0
        )

    def own_d(owner):
        return own(tab_d, part_d, owner)

    def own_a(owner):
        return own(tab_a, part_a, owner)

    def smoothing():
        for k in range(num_tiles):
            x = vol_out[k]
            step = pltpu.roll(x, slices - 1, 0) - x
            slope = jnp.clip(step, -HUBER_DELTA, HUBER_DELTA)
            slope = jnp.where(slice_index < slices - 1, slope, 0.0)
            smooth[k] = pltpu.roll(slope, 1, 0) - slope

    parts = 4
    per = slots_a // parts if slots_a % parts == 0 else slots_a

    def pieces(fn):
        return [functools.partial(fn, i * per, per) for i in range(slots_a // per)]

    def twin_part():
        return remote(twin_s, twin_r, tw_s.at[0], tw_r.at[0], twin)

    def across_part(k):
        return remote(send_a.at[k], recv_a.at[k], ca_s.at[k], ca_r.at[k], cdev(k))

    def across_out(k):
        return remote(gat_a.at[c], gat_a.at[c], cg_s.at[k], cg_r.at[k], cdev(k))

    def twin_out(k):
        shard = gat_a.at[ccol(chips - k, core)]
        return remote(shard, shard, tg_s.at[k], tg_r.at[k], twin)

    def each_chip(first, fn):
        def one(k, carry):
            fn(k)
            return carry

        lax.fori_loop(first, chips, one, 0)

    def start_across():
        def stage(k):
            twin_s[k] = own_a(ccol(k, 1 - core)).astype(BF16)

        each_chip(0, stage)
        twin_part().start()

    def send_across():
        twin_part().wait_recv()

        def stage(k):
            send_a[k] = (own_a(ccol(k, core)) + twin_r[k].astype(F32)).astype(BF16)
            across_part(k).start()

        each_chip(1, stage)

    def finish_across():
        def one(k, total):
            across_part(k).wait_recv()
            return total + recv_a[k].astype(F32)

        projection = lax.fori_loop(1, chips, one, own_a(c) + twin_r[0].astype(F32))
        residual = wt_a[...] * (meas_a[...] - projection)
        res_a[...] = residual
        gat_a[c] = residual.astype(BF16)
        each_chip(1, lambda k: across_out(k).start())
        twin_out(0).start()

    def pass_across():
        def relay(k):
            across_out(k).wait_recv()
            twin_out(k).start()

        each_chip(1, relay)

    def collect_across():
        each_chip(0, lambda k: twin_out(k).wait_recv())

    def drain_across():
        def one(k):
            across_part(k).wait_send()
            across_out(k).wait_send()

        each_chip(1, one)
        each_chip(0, lambda k: twin_out(k).wait_send())
        twin_part().wait_send()

    def plus(t, k):
        return remote(sp.at[t, k], rp.at[t, k], sp_s.at[t, k], sp_r.at[t, k], zdev(1))

    def minus(t, k):
        return remote(sm.at[t, k], rm.at[t, k], sm_s.at[t, k], sm_r.at[t, k], zdev(-1))

    def half(i):
        return remote(half_s.at[i], half_r.at[i], h_s.at[i], h_r.at[i], zdev(gap if i == 0 else -gap))

    def full(i):
        return remote(full_s.at[i], full_r.at[i], f_s.at[i], f_r.at[i], zdev(gap if i == 0 else -gap))

    def chain_step(t, k):
        value = own_d(zrow(up_steps - t + gap * k))
        if t:
            plus(t - 1, k).wait_recv()
            value = value + rp[t - 1, k].astype(F32)
        sp[t, k] = value.astype(BF16)
        plus(t, k).start()
        if t < down_steps:
            value = own_d(zrow(t - down_steps + gap * k))
            if t:
                minus(t - 1, k).wait_recv()
                value = value + rm[t - 1, k].astype(F32)
            sm[t, k] = value.astype(BF16)
            minus(t, k).start()

    def hub_total(k):
        value = own_d(zrow(gap * k))
        if down_steps:
            minus(down_steps - 1, k).wait_recv()
            value = value + rm[down_steps - 1, k].astype(F32)
        plus(up_steps - 1, k).wait_recv()
        return value + rp[up_steps - 1, k].astype(F32)

    def reduce_down(fillers):
        fillers = list(fillers)
        for t in range(up_steps):
            for k in (2, 1, 3):
                chain_step(t, k)
            if fillers:
                fillers.pop(0)()
        value = hub_total(2)
        half_s[0] = value[:, :lanes].astype(BF16)
        half_s[1] = value[:, lanes:].astype(BF16)
        half(0).start()
        half(1).start()
        for filler in fillers:
            filler()
        start_across()
        chain_step(0, 0)
        hub[0] = hub_total(1)
        hub[1] = hub_total(3)
        if up_steps > 2:
            chain_step(1, 0)
        send_across()
        for t in range(2 if up_steps > 2 else 1, up_steps - 1):
            chain_step(t, 0)
        half(0).wait_recv()
        value = hub[0]
        full_s[0, :, :lanes] = (value[:, :lanes] + half_r[0].astype(F32)).astype(BF16)
        full_s[0, :, lanes:] = value[:, lanes:].astype(BF16)
        full(0).start()
        half(1).wait_recv()
        value = hub[1]
        full_s[1, :, :lanes] = value[:, :lanes].astype(BF16)
        full_s[1, :, lanes:] = (value[:, lanes:] + half_r[1].astype(F32)).astype(BF16)
        full(1).start()
        if up_steps > 1:
            chain_step(up_steps - 1, 0)
        smoothing()
        hub[2] = hub_total(0)
        finish_across()
        full(0).wait_recv()
        full(1).wait_recv()
        projection = hub[2] + full_r[0].astype(F32) + full_r[1].astype(F32)
        residual = wt_d[...] * (meas_d[...] - projection)
        res_d[...] = residual
        gat_d[z] = residual.astype(BF16)

    def out_full(i, offset):
        mine = gat_d.at[zrow(offset)]
        return remote(mine, mine, gf_s.at[i], gf_r.at[i], zdev(gap if i == 0 else -gap))

    def out_half(i):
        owner = zrow(-gap if i == 0 else gap)
        piece = gat_d.at[owner, :, pl.ds(i * lanes, lanes)]
        return remote(piece, piece, gh_s.at[i], gh_r.at[i], zdev(gap if i == 0 else -gap))

    def out_minus(t, k):
        shard = gat_d.at[zrow(t + gap * k)]
        return remote(shard, shard, gm_s.at[t, k], gm_r.at[t, k], zdev(-1))

    def out_plus(t, k):
        shard = gat_d.at[zrow(gap * k - t)]
        return remote(shard, shard, gp_s.at[t, k], gp_r.at[t, k], zdev(1))

    def out_step(t, k):
        if t:
            out_minus(t - 1, k).wait_recv()
        out_minus(t, k).start()
        if t < down_steps:
            if t:
                out_plus(t - 1, k).wait_recv()
            out_plus(t, k).start()

    def out_last(k):
        out_minus(up_steps - 1, k).wait_recv()
        if down_steps:
            out_plus(down_steps - 1, k).wait_recv()

    def spread_down(fillers):
        fillers = list(fillers)
        out_full(0, 0).start()
        out_full(1, 0).start()
        for t in range(up_steps - 1):
            out_step(t, 0)
        out_full(0, 0).wait_recv()
        out_half(0).start()
        out_full(1, 0).wait_recv()
        out_half(1).start()
        for k in (1, 3):
            out_step(0, k)
        out_step(up_steps - 1, 0)
        for t in range(1, up_steps):
            for k in (1, 3):
                out_step(t, k)
        out_half(0).wait_recv()
        out_half(1).wait_recv()
        for t in range(up_steps):
            out_step(t, 2)
            if t == 0:
                pass_across()
            if t == min(1, up_steps - 1):
                collect_across()
            if t >= 1:
                fillers.pop(0)()
        for filler in fillers:
            filler()
        for k in (0, 1, 3, 2):
            out_last(k)

    def drain_down():
        for k in range(RING):
            for t in range(up_steps):
                plus(t, k).wait_send()
                out_minus(t, k).wait_send()
            for t in range(down_steps):
                minus(t, k).wait_send()
                out_plus(t, k).wait_send()
        for i in range(2):
            half(i).wait_send()
            full(i).wait_send()
            out_full(i, 0).wait_send()
            out_half(i).wait_send()

    loads[0].wait()
    loads[1].wait()
    forward(tab_d, blk_d, part_d, 0, slots_d)
    for load in loads[2:]:
        load.wait()
    pl.semaphore_wait(barrier, chips + 4)

    def iteration(step, carry):
        reduce_down(pieces(functools.partial(forward, tab_a, blk_a, part_a)))
        spread_down(pieces(functools.partial(backward, tab_a, blk_a, gat_a, cum_a)))
        backward(tab_d, blk_d, gat_d, cum_d, 0, slots_d)
        for k in range(num_tiles):
            gradient = cum_a[tab_a[LAST, k]] + cum_d[tab_d[LAST, k]]
            x = vol_out[k]
            vol_out[k] = jnp.maximum(
                x + STEP_SIZE * (gradient - SMOOTH_WEIGHT * smooth[k]), 0.0
            )
        drain_across()
        drain_down()

        @pl.when(step < ITERS - 1)
        def _():
            forward(tab_d, blk_d, part_d, 0, slots_d)

        return carry

    lax.fori_loop(0, ITERS, iteration, 0)


def shards(
    n_row,
    n_col,
    volume,
    blocks_across,
    downward_ray_blocks,
    tiles_across,
    tiles_down,
    footprint_across,
    footprint_down,
    rays_across,
    rays_down,
    owners_across,
    owners_down,
    observed_sinogram_across,
    observed_sinogram_down,
    weights_across,
    weights_down,
):
    voxels = volume[0, 0]
    num_tiles, slices, tile = voxels.shape
    slots_a, _, rays = blocks_across.shape
    slots_d = downward_ray_blocks.shape[0]
    rows = OWNED * slices
    if slots_a == slots_d and owners_across.shape == owners_down.shape:
        tab_a, tab_d = jax.vmap(functools.partial(slot_tables, num_tiles))(
            jnp.concatenate([rays_across[0], rays_down[0]]),
            jnp.concatenate([owners_across, owners_down]),
            jnp.concatenate([tiles_across[0], tiles_down[0]]),
            jnp.concatenate([footprint_across[0], footprint_down[0]]),
        )
    else:
        tab_a = slot_tables(
            num_tiles, rays_across[0, 0], owners_across[0], tiles_across[0, 0], footprint_across[0, 0]
        )
        tab_d = slot_tables(
            num_tiles, rays_down[0, 0], owners_down[0], tiles_down[0, 0], footprint_down[0, 0]
        )
    chips = n_col // 2
    gap = n_row // RING
    up_steps = gap // 2
    down_steps = max(gap // 2 - 1, 1)
    dma = pltpu.SemaphoreType.DMA

    def shard(*lead):
        return pltpu.VMEM((*lead, rows, rays), BF16)

    vmem = pl.BlockSpec(memory_space=pltpu.VMEM)
    smem = pl.BlockSpec(memory_space=pltpu.SMEM)
    hbm = pl.BlockSpec(memory_space=pltpu.HBM)
    own_shape = jax.ShapeDtypeStruct((rows, rays), F32)
    outs = pl.pallas_call(
        functools.partial(body, n_row, n_col),
        out_shape=(jax.ShapeDtypeStruct(voxels.shape, F32), own_shape, own_shape),
        in_specs=[smem, smem] + [hbm] * 7,
        out_specs=(vmem, vmem, vmem),
        scratch_shapes=[
            pltpu.VMEM(blocks_across.shape, BF16),
            pltpu.VMEM(downward_ray_blocks.shape, BF16),
            pltpu.VMEM((rows, rays), F32),
            pltpu.VMEM((rows, rays), F32),
            pltpu.VMEM((rows, rays), F32),
            pltpu.VMEM((rows, rays), F32),
            pltpu.VMEM((slots_a + 1, slices, rays), F32),
            pltpu.VMEM((slots_d + 1, slices, rays), F32),
            pltpu.VMEM((slots_a + 1, slices, tile), F32),
            pltpu.VMEM((slots_d + 1, slices, tile), F32),
            pltpu.VMEM(voxels.shape, F32),
            shard(n_col),
            shard(n_row),
            shard(chips),
            shard(chips),
            shard(chips),
            shard(chips),
            shard(up_steps, RING),
            shard(up_steps, RING),
            shard(down_steps, RING),
            shard(down_steps, RING),
            pltpu.VMEM((3, rows, rays), F32),
            pltpu.VMEM((2, rows, rays // 2), BF16),
            pltpu.VMEM((2, rows, rays // 2), BF16),
            shard(2),
            shard(2),
            dma((7,)),
            dma((1,)),
            dma((1,)),
            dma((chips,)),
            dma((chips,)),
            dma((chips,)),
            dma((chips,)),
            dma((chips,)),
            dma((chips,)),
            dma((up_steps, RING)),
            dma((up_steps, RING)),
            dma((down_steps, RING)),
            dma((down_steps, RING)),
            dma((2,)),
            dma((2,)),
            dma((2,)),
            dma((2,)),
            dma((2,)),
            dma((2,)),
            dma((2,)),
            dma((2,)),
            dma((down_steps, RING)),
            dma((down_steps, RING)),
            dma((up_steps, RING)),
            dma((up_steps, RING)),
        ],
        compiler_params=pltpu.CompilerParams(
            collective_id=0, has_side_effects=True, vmem_limit_bytes=67000000
        ),
        name="tomography",
    )(
        tab_a,
        tab_d,
        voxels,
        blocks_across,
        downward_ray_blocks,
        observed_sinogram_across.reshape(rows, rays),
        observed_sinogram_down.reshape(rows, rays),
        weights_across.reshape(rows, rays),
        weights_down.reshape(rows, rays),
    )
    shape = observed_sinogram_across.shape
    return (outs[0][None, None], outs[1].reshape(shape), outs[2].reshape(shape))


def solution(mesh):
    return jax.shard_map(
        functools.partial(shards, mesh.shape["row"], mesh.shape["col"]),
        mesh=mesh,
        in_specs=(
            P("row", "col", None, None, None),
            P(),
            P(),
            P("row", "col", None),
            P("row", "col", None),
            P("row", "col", None),
            P("row", "col", None),
            P("row", "col", None),
            P("row", "col", None),
            P("row", None),
            P("col", None),
            P("row", "col", None, None, None),
            P("row", "col", None, None, None),
            P("row", "col", None, None, None),
            P("row", "col", None, None, None),
        ),
        out_specs=(
            P("row", "col", None, None, None),
            P("row", "col", None, None, None),
            P("row", "col", None, None, None),
        ),
        check_vma=False,
    )
```

```python
import functools

import jax
import jax.numpy as jnp
from jax import lax
from jax.experimental import pallas as pl
from jax.experimental.pallas import tpu as pltpu
from jax.sharding import PartitionSpec as P

OWNED = 2
ITERS = 2
RING = 4

HUBER_DELTA = 0.5
STEP_SIZE = 0.05
SMOOTH_WEIGHT = 1.0

F32 = jnp.float32
BF16 = jnp.bfloat16

SLOT, TILE_OF, FOOT, OWNER, ODD, SAME, INVERSE, LAST = range(8)


def slot_tables(num_tiles, ray_list, owner_row, tiles, footprint):
    positions = owner_row.shape[0]
    slots = ray_list.shape[0]
    ids = jnp.arange(slots, dtype=jnp.int32)
    earlier = ids[None, :] < ids[:, None]
    before = (tiles[None, :] < tiles[:, None]) | ((tiles[None, :] == tiles[:, None]) & earlier)
    rank = jnp.sum(before.astype(jnp.int32), axis=1)
    named = ray_list[:, None] == jnp.arange(positions, dtype=jnp.int32)[None, :]
    position = jnp.sum(jnp.where(named, owner_row[None, :], 0), axis=1)
    here = rank[None, :] == ids[:, None]

    def sort(values):
        return jnp.sum(jnp.where(here, values[None, :], 0), axis=1)

    slot = sort(ids)
    tile = sort(tiles)
    foot = sort(footprint)
    pos = sort(position)
    same = jnp.concatenate([jnp.zeros((1,), jnp.int32), (tile[1:] == tile[:-1]).astype(jnp.int32)])
    holds = pos[None, :] == jnp.arange(positions, dtype=jnp.int32)[:, None]
    inverse = slots - jnp.sum(jnp.where(holds, slots - ids[None, :], 0), axis=1)
    tile_ids = jnp.arange(num_tiles, dtype=jnp.int32)
    upto = jnp.sum((tiles[None, :] <= tile_ids[:, None]).astype(jnp.int32), axis=1)
    present = jnp.any(tiles[None, :] == tile_ids[:, None], axis=1)
    last = jnp.where(present, upto - 1, slots)
    width = max(positions, slots, num_tiles)

    def row(values):
        return jnp.pad(values.astype(jnp.int32), (0, width - values.shape[0]))

    return jnp.stack(
        [row(v) for v in (slot, tile, foot, pos // OWNED, pos % OWNED, same, inverse, last)]
    )


def body(
    n_row,
    n_col,
    tab_a,
    tab_d,
    vol,
    blk_a_hbm,
    blk_d_hbm,
    meas_a_hbm,
    meas_d_hbm,
    wt_a_hbm,
    wt_d_hbm,
    vol_out,
    res_a,
    res_d,
    blk_a,
    blk_d,
    meas_a,
    meas_d,
    wt_a,
    wt_d,
    part_a,
    part_d,
    cum_a,
    cum_d,
    smooth,
    gat_a,
    gat_d,
    twin_s,
    twin_r,
    send_a,
    recv_a,
    sp,
    rp,
    sm,
    rm,
    hub,
    half_s,
    half_r,
    full_s,
    full_r,
    blk_sem,
    tw_s,
    tw_r,
    tg_s,
    tg_r,
    ca_s,
    ca_r,
    cg_s,
    cg_r,
    sp_s,
    sp_r,
    sm_s,
    sm_r,
    h_s,
    h_r,
    f_s,
    f_r,
    gf_s,
    gf_r,
    gh_s,
    gh_r,
    gp_s,
    gp_r,
    gm_s,
    gm_r,
):
    z = lax.axis_index("row")
    c = lax.axis_index("col")
    num_tiles, slices, _ = vol.shape
    slots_a = blk_a.shape[0]
    slots_d = blk_d.shape[0]
    rays = blk_a.shape[2]
    lanes = rays // 2
    gap = n_row // RING
    up_steps = gap // 2
    down_steps = gap // 2 - 1

    def zrow(offset):
        return lax.rem(z + (offset % n_row), n_row)

    def zdev(offset):
        return (zrow(offset), c)

    chips = n_col // 2
    core = lax.rem(c, 2)
    chip = (c - core) // 2
    twin = (z, c + 1 - 2 * core)

    def ccol(k, side):
        return 2 * lax.rem(chip + k, chips) + side

    def cdev(k):
        return (z, ccol(k, core))

    def remote(src, dst, s_sem, r_sem, dev):
        return pltpu.make_async_remote_copy(
            src_ref=src,
            dst_ref=dst,
            send_sem=s_sem,
            recv_sem=r_sem,
            device_id=dev,
            device_id_type=pl.DeviceIdType.MESH,
        )

    pairs = (
        (vol, vol_out),
        (blk_d_hbm, blk_d),
        (blk_a_hbm, blk_a),
        (meas_d_hbm, meas_d),
        (wt_d_hbm, wt_d),
        (meas_a_hbm, meas_a),
        (wt_a_hbm, wt_a),
    )
    loads = [pltpu.make_async_copy(src, dst, blk_sem.at[i]) for i, (src, dst) in enumerate(pairs)]
    for load in loads:
        load.start()

    barrier = pltpu.get_barrier_semaphore()

    def greet(k, carry):
        pl.semaphore_signal(
            barrier, inc=1, device_id=cdev(k), device_id_type=pl.DeviceIdType.MESH
        )
        return carry

    for offset in (gap, -gap, 1, -1):
        pl.semaphore_signal(
            barrier, inc=1, device_id=zdev(offset), device_id_type=pl.DeviceIdType.MESH
        )
    pl.semaphore_signal(barrier, inc=1, device_id=twin, device_id_type=pl.DeviceIdType.MESH)
    lax.fori_loop(1, chips, greet, 0)

    zero = jnp.zeros((slices, rays), F32)
    part_a[slots_a] = zero
    part_d[slots_d] = zero
    cum_a[slots_a] = zero
    cum_d[slots_d] = zero

    ray_index = lax.broadcasted_iota(jnp.int32, (slices, rays), 1)
    slice_index = lax.broadcasted_iota(jnp.int32, (slices, rays), 0)

    def forward(tab, blk, part, first, count):
        def one(j, carry):
            tile = vol_out[tab[TILE_OF, j]].astype(BF16)
            value = jnp.dot(tile, blk[tab[SLOT, j]], preferred_element_type=F32)
            part[j] = jnp.where(ray_index < tab[FOOT, j], value, 0.0)
            return carry

        lax.fori_loop(first, first + count, one, 0, unroll=min(4, count))

    def backward(tab, blk, gat, cum, first, count):
        def one(j, total):
            both = gat[tab[OWNER, j]].astype(F32)
            items = jnp.where(tab[ODD, j] == 1, both[slices:], both[:slices])
            items = jnp.where(ray_index < tab[FOOT, j], items, 0.0).astype(BF16)
            value = lax.dot_general(
                items, blk[tab[SLOT, j]], (((1,), (1,)), ((), ())), preferred_element_type=F32
            )
            total = jnp.where(tab[SAME, j] == 1, total, 0.0) + value
            cum[j] = total
            return total

        start = cum[first - 1] if first else zero
        lax.fori_loop(first, first + count, one, start, unroll=min(4, count))

    def own(tab, part, owner):
        return jnp.concatenate(
            [part[tab[INVERSE, 2 * owner]], part[tab[INVERSE, 2 * owner + 1]]], axis=0
        )

    def own_d(owner):
        return own(tab_d, part_d, owner)

    def own_a(owner):
        return own(tab_a, part_a, owner)

    def smoothing():
        for k in range(num_tiles):
            x = vol_out[k]
            step = pltpu.roll(x, slices - 1, 0) - x
            slope = jnp.clip(step, -HUBER_DELTA, HUBER_DELTA)
            slope = jnp.where(slice_index < slices - 1, slope, 0.0)
            smooth[k] = pltpu.roll(slope, 1, 0) - slope

    parts = 4
    per = slots_a // parts if slots_a % parts == 0 else slots_a

    def pieces(fn):
        return [functools.partial(fn, i * per, per) for i in range(slots_a // per)]

    def twin_part():
        return remote(twin_s, twin_r, tw_s.at[0], tw_r.at[0], twin)

    def across_part(k):
        return remote(send_a.at[k], recv_a.at[k], ca_s.at[k], ca_r.at[k], cdev(k))

    def across_out(k):
        return remote(gat_a.at[c], gat_a.at[c], cg_s.at[k], cg_r.at[k], cdev(k))

    def twin_out(k):
        shard = gat_a.at[ccol(chips - k, core)]
        return remote(shard, shard, tg_s.at[k], tg_r.at[k], twin)

    def each_chip(first, fn):
        def one(k, carry):
            fn(k)
            return carry

        lax.fori_loop(first, chips, one, 0)

    def start_across():
        def stage(k):
            twin_s[k] = own_a(ccol(k, 1 - core)).astype(BF16)

        each_chip(0, stage)
        twin_part().start()

    def send_across():
        twin_part().wait_recv()

        def stage(k):
            send_a[k] = (own_a(ccol(k, core)) + twin_r[k].astype(F32)).astype(BF16)
            across_part(k).start()

        each_chip(1, stage)

    def finish_across():
        def one(k, total):
            across_part(k).wait_recv()
            return total + recv_a[k].astype(F32)

        projection = lax.fori_loop(1, chips, one, own_a(c) + twin_r[0].astype(F32))
        residual = wt_a[...] * (meas_a[...] - projection)
        res_a[...] = residual
        gat_a[c] = residual.astype(BF16)
        each_chip(1, lambda k: across_out(k).start())
        twin_out(0).start()

    def pass_across():
        def relay(k):
            across_out(k).wait_recv()
            twin_out(k).start()

        each_chip(1, relay)

    def collect_across():
        each_chip(0, lambda k: twin_out(k).wait_recv())

    def drain_across():
        def one(k):
            across_part(k).wait_send()
            across_out(k).wait_send()

        each_chip(1, one)
        each_chip(0, lambda k: twin_out(k).wait_send())
        twin_part().wait_send()

    def plus(t, k):
        return remote(sp.at[t, k], rp.at[t, k], sp_s.at[t, k], sp_r.at[t, k], zdev(1))

    def minus(t, k):
        return remote(sm.at[t, k], rm.at[t, k], sm_s.at[t, k], sm_r.at[t, k], zdev(-1))

    def half(i):
        return remote(half_s.at[i], half_r.at[i], h_s.at[i], h_r.at[i], zdev(gap if i == 0 else -gap))

    def full(i):
        return remote(full_s.at[i], full_r.at[i], f_s.at[i], f_r.at[i], zdev(gap if i == 0 else -gap))

    def chain_step(t, k):
        value = own_d(zrow(up_steps - t + gap * k))
        if t:
            plus(t - 1, k).wait_recv()
            value = value + rp[t - 1, k].astype(F32)
        sp[t, k] = value.astype(BF16)
        plus(t, k).start()
        if t < down_steps:
            value = own_d(zrow(t - down_steps + gap * k))
            if t:
                minus(t - 1, k).wait_recv()
                value = value + rm[t - 1, k].astype(F32)
            sm[t, k] = value.astype(BF16)
            minus(t, k).start()

    def hub_total(k):
        value = own_d(zrow(gap * k))
        if down_steps:
            minus(down_steps - 1, k).wait_recv()
            value = value + rm[down_steps - 1, k].astype(F32)
        plus(up_steps - 1, k).wait_recv()
        return value + rp[up_steps - 1, k].astype(F32)

    def reduce_down(fillers):
        fillers = list(fillers)
        for t in range(up_steps):
            for k in (2, 1, 3):
                chain_step(t, k)
            if fillers:
                fillers.pop(0)()
        value = hub_total(2)
        half_s[0] = value[:, :lanes].astype(BF16)
        half_s[1] = value[:, lanes:].astype(BF16)
        half(0).start()
        half(1).start()
        for filler in fillers:
            filler()
        start_across()
        chain_step(0, 0)
        hub[0] = hub_total(1)
        hub[1] = hub_total(3)
        if up_steps > 2:
            chain_step(1, 0)
        send_across()
        for t in range(2 if up_steps > 2 else 1, up_steps - 1):
            chain_step(t, 0)
        half(0).wait_recv()
        value = hub[0]
        full_s[0, :, :lanes] = (value[:, :lanes] + half_r[0].astype(F32)).astype(BF16)
        full_s[0, :, lanes:] = value[:, lanes:].astype(BF16)
        full(0).start()
        half(1).wait_recv()
        value = hub[1]
        full_s[1, :, :lanes] = value[:, :lanes].astype(BF16)
        full_s[1, :, lanes:] = (value[:, lanes:] + half_r[1].astype(F32)).astype(BF16)
        full(1).start()
        if up_steps > 1:
            chain_step(up_steps - 1, 0)
        smoothing()
        hub[2] = hub_total(0)
        full(0).wait_recv()
        full(1).wait_recv()
        projection = hub[2] + full_r[0].astype(F32) + full_r[1].astype(F32)
        residual = wt_d[...] * (meas_d[...] - projection)
        res_d[...] = residual
        gat_d[z] = residual.astype(BF16)

    def out_full(i, offset):
        mine = gat_d.at[zrow(offset)]
        return remote(mine, mine, gf_s.at[i], gf_r.at[i], zdev(gap if i == 0 else -gap))

    def out_half(i):
        owner = zrow(-gap if i == 0 else gap)
        piece = gat_d.at[owner, :, pl.ds(i * lanes, lanes)]
        return remote(piece, piece, gh_s.at[i], gh_r.at[i], zdev(gap if i == 0 else -gap))

    def out_minus(t, k):
        shard = gat_d.at[zrow(t + gap * k)]
        return remote(shard, shard, gm_s.at[t, k], gm_r.at[t, k], zdev(-1))

    def out_plus(t, k):
        shard = gat_d.at[zrow(gap * k - t)]
        return remote(shard, shard, gp_s.at[t, k], gp_r.at[t, k], zdev(1))

    def out_step(t, k):
        if t:
            out_minus(t - 1, k).wait_recv()
        out_minus(t, k).start()
        if t < down_steps:
            if t:
                out_plus(t - 1, k).wait_recv()
            out_plus(t, k).start()

    def out_last(k):
        out_minus(up_steps - 1, k).wait_recv()
        if down_steps:
            out_plus(down_steps - 1, k).wait_recv()

    def spread_down(fillers):
        fillers = list(fillers)
        out_full(0, 0).start()
        out_full(1, 0).start()
        out_step(0, 0)
        finish_across()
        for t in range(1, up_steps - 1):
            out_step(t, 0)
        out_full(0, 0).wait_recv()
        out_half(0).start()
        out_full(1, 0).wait_recv()
        out_half(1).start()
        for k in (1, 3):
            out_step(0, k)
        if up_steps > 1:
            out_step(up_steps - 1, 0)
        for t in range(1, up_steps - 1):
            for k in (1, 3):
                out_step(t, k)
        out_half(0).wait_recv()
        out_half(1).wait_recv()
        for t in range(up_steps):
            out_step(t, 2)
            if t == 0 and up_steps > 1:
                for k in (1, 3):
                    out_step(up_steps - 1, k)
            if t == 0:
                pass_across()
            if t == min(1, up_steps - 1):
                collect_across()
            if t >= 1:
                fillers.pop(0)()
        for filler in fillers:
            filler()
        for k in (0, 1, 3, 2):
            out_last(k)

    def drain_down():
        for k in range(RING):
            for t in range(up_steps):
                plus(t, k).wait_send()
                out_minus(t, k).wait_send()
            for t in range(down_steps):
                minus(t, k).wait_send()
                out_plus(t, k).wait_send()
        for i in range(2):
            half(i).wait_send()
            full(i).wait_send()
            out_full(i, 0).wait_send()
            out_half(i).wait_send()

    loads[0].wait()
    loads[1].wait()
    forward(tab_d, blk_d, part_d, 0, slots_d)
    for load in loads[2:]:
        load.wait()
    pl.semaphore_wait(barrier, chips + 4)

    def iteration(step, carry):
        reduce_down(pieces(functools.partial(forward, tab_a, blk_a, part_a)))
        spread_down(pieces(functools.partial(backward, tab_a, blk_a, gat_a, cum_a)))
        backward(tab_d, blk_d, gat_d, cum_d, 0, slots_d)
        for k in range(num_tiles):
            gradient = cum_a[tab_a[LAST, k]] + cum_d[tab_d[LAST, k]]
            x = vol_out[k]
            vol_out[k] = jnp.maximum(
                x + STEP_SIZE * (gradient - SMOOTH_WEIGHT * smooth[k]), 0.0
            )
        drain_across()
        drain_down()

        @pl.when(step < ITERS - 1)
        def _():
            forward(tab_d, blk_d, part_d, 0, slots_d)

        return carry

    lax.fori_loop(0, ITERS, iteration, 0)


def shards(
    n_row,
    n_col,
    volume,
    blocks_across,
    downward_ray_blocks,
    tiles_across,
    tiles_down,
    footprint_across,
    footprint_down,
    rays_across,
    rays_down,
    owners_across,
    owners_down,
    observed_sinogram_across,
    observed_sinogram_down,
    weights_across,
    weights_down,
):
    voxels = volume[0, 0]
    num_tiles, slices, tile = voxels.shape
    slots_a, _, rays = blocks_across.shape
    slots_d = downward_ray_blocks.shape[0]
    rows = OWNED * slices
    if slots_a == slots_d and owners_across.shape == owners_down.shape:
        tab_a, tab_d = jax.vmap(functools.partial(slot_tables, num_tiles))(
            jnp.concatenate([rays_across[0], rays_down[0]]),
            jnp.concatenate([owners_across, owners_down]),
            jnp.concatenate([tiles_across[0], tiles_down[0]]),
            jnp.concatenate([footprint_across[0], footprint_down[0]]),
        )
    else:
        tab_a = slot_tables(
            num_tiles, rays_across[0, 0], owners_across[0], tiles_across[0, 0], footprint_across[0, 0]
        )
        tab_d = slot_tables(
            num_tiles, rays_down[0, 0], owners_down[0], tiles_down[0, 0], footprint_down[0, 0]
        )
    chips = n_col // 2
    gap = n_row // RING
    up_steps = gap // 2
    down_steps = max(gap // 2 - 1, 1)
    dma = pltpu.SemaphoreType.DMA

    def shard(*lead):
        return pltpu.VMEM((*lead, rows, rays), BF16)

    vmem = pl.BlockSpec(memory_space=pltpu.VMEM)
    smem = pl.BlockSpec(memory_space=pltpu.SMEM)
    hbm = pl.BlockSpec(memory_space=pltpu.HBM)
    own_shape = jax.ShapeDtypeStruct((rows, rays), F32)
    outs = pl.pallas_call(
        functools.partial(body, n_row, n_col),
        out_shape=(jax.ShapeDtypeStruct(voxels.shape, F32), own_shape, own_shape),
        in_specs=[smem, smem] + [hbm] * 7,
        out_specs=(vmem, vmem, vmem),
        scratch_shapes=[
            pltpu.VMEM(blocks_across.shape, BF16),
            pltpu.VMEM(downward_ray_blocks.shape, BF16),
            pltpu.VMEM((rows, rays), F32),
            pltpu.VMEM((rows, rays), F32),
            pltpu.VMEM((rows, rays), F32),
            pltpu.VMEM((rows, rays), F32),
            pltpu.VMEM((slots_a + 1, slices, rays), F32),
            pltpu.VMEM((slots_d + 1, slices, rays), F32),
            pltpu.VMEM((slots_a + 1, slices, tile), F32),
            pltpu.VMEM((slots_d + 1, slices, tile), F32),
            pltpu.VMEM(voxels.shape, F32),
            shard(n_col),
            shard(n_row),
            shard(chips),
            shard(chips),
            shard(chips),
            shard(chips),
            shard(up_steps, RING),
            shard(up_steps, RING),
            shard(down_steps, RING),
            shard(down_steps, RING),
            pltpu.VMEM((3, rows, rays), F32),
            pltpu.VMEM((2, rows, rays // 2), BF16),
            pltpu.VMEM((2, rows, rays // 2), BF16),
            shard(2),
            shard(2),
            dma((7,)),
            dma((1,)),
            dma((1,)),
            dma((chips,)),
            dma((chips,)),
            dma((chips,)),
            dma((chips,)),
            dma((chips,)),
            dma((chips,)),
            dma((up_steps, RING)),
            dma((up_steps, RING)),
            dma((down_steps, RING)),
            dma((down_steps, RING)),
            dma((2,)),
            dma((2,)),
            dma((2,)),
            dma((2,)),
            dma((2,)),
            dma((2,)),
            dma((2,)),
            dma((2,)),
            dma((down_steps, RING)),
            dma((down_steps, RING)),
            dma((up_steps, RING)),
            dma((up_steps, RING)),
        ],
        compiler_params=pltpu.CompilerParams(
            collective_id=0, has_side_effects=True, vmem_limit_bytes=66000000
        ),
        name="tomography",
    )(
        tab_a,
        tab_d,
        voxels,
        blocks_across,
        downward_ray_blocks,
        observed_sinogram_across.reshape(rows, rays),
        observed_sinogram_down.reshape(rows, rays),
        weights_across.reshape(rows, rays),
        weights_down.reshape(rows, rays),
    )
    shape = observed_sinogram_across.shape
    return (outs[0][None, None], outs[1].reshape(shape), outs[2].reshape(shape))


def solution(mesh):
    return jax.shard_map(
        functools.partial(shards, mesh.shape["row"], mesh.shape["col"]),
        mesh=mesh,
        in_specs=(
            P("row", "col", None, None, None),
            P(),
            P(),
            P("row", "col", None),
            P("row", "col", None),
            P("row", "col", None),
            P("row", "col", None),
            P("row", "col", None),
            P("row", "col", None),
            P("row", None),
            P("col", None),
            P("row", "col", None, None, None),
            P("row", "col", None, None, None),
            P("row", "col", None, None, None),
            P("row", "col", None, None, None),
        ),
        out_specs=(
            P("row", "col", None, None, None),
            P("row", "col", None, None, None),
            P("row", "col", None, None, None),
        ),
        check_vma=False,
    )
```
